256 devices in a mesh: mem: 8 (over z), reg: 32 (over y, x, core).
Axes of the slice: x: 4, y: 4, z: 8, core: 2. Of those that a mesh axis runs over, the one named last changes fastest.
Arguments:
- member_values: float32 [80, 524288], P('mem', 'reg'), may hold values from -6 to 6
- obs_value: float32 [524288], P('reg'), may hold values from -6 to 6
- obs_weight: float32 [524288], P('reg'), may hold values from 0.25 to 4
- obs_cell: int32 [524288], P('reg'), may hold values from -1 to 61439, as said below
Outputs:
- deviation: float32 [80, 61440], P('mem', 'reg')
- departure: float32 [61440], P('reg')
- variance: float32 [61440], P('reg')
- error_variance: float32 [61440], P('reg')
- obs_total: int32 [61440], P('reg')
The draws below stay inside these ranges and needn't reach their ends.
Inputs may be any that keep to these rules, and one draw needn't show every extreme that they name: `obs_cell`: cell c is owned by region c // 1920. The 16384 slots of one region are 32 blocks of 512 slots, block r holding only cells owned by region r, live slots first and -1 in the empty ones. Every block has at least 128 live slots; one owner's block is full in every region.
All inputs are finite; a program needn't handle non-finite values.
Results may differ from the reference program's by a relative error of at most 0.0003.
Values sent between devices are 32-bit elements; how exact they have to be, the bound alone decides.
A program may use at most 64 MiB of HBM per device.

```python
import math
import jax
import jax.numpy as jnp

CAP = 512
CELL_DEV = 1920
MEMBERS = 80
OBS = 524288
CELLS = 61440
N_REG = 32


def draw_obs_cell(key, part):
    subkeys = jax.random.split(jax.random.fold_in(key, 7), 4)
    dense_owner = jax.random.randint(subkeys[0], (), 0, N_REG)
    block_counts = jax.random.randint(subkeys[1], (N_REG, N_REG), CAP // 4, CAP + 1)
    owner_ids = jnp.arange(N_REG, dtype=jnp.int32)
    block_counts = jnp.where(owner_ids[None, :] == dense_owner, CAP, block_counts)
    slot_ids = jnp.arange(CAP, dtype=jnp.int32)
    live = slot_ids[None, None, :] < block_counts[:, :, None]
    factor_one = jax.random.randint(subkeys[2], (N_REG, N_REG, CAP), 0, CELL_DEV)
    factor_two = jax.random.randint(subkeys[3], (N_REG, N_REG, CAP), 0, CELL_DEV)
    local_cell = factor_one * factor_two // CELL_DEV
    local_cell = (local_cell * 7919 + 101) % CELL_DEV
    cell_ids = owner_ids[None, :, None] * CELL_DEV + local_cell
    cell_ids = jnp.where(live, cell_ids, -1)
    return cell_ids.reshape(-1).astype(jnp.int32)


def levels(rng, extent, pieces, least, largest):
    def one(position, shards_of):
        draws = jax.random.uniform(jax.random.fold_in(jax.random.fold_in(rng, 6), position), (shards_of,), jnp.float32, least / len(pieces), largest / len(pieces))
        return jnp.repeat(jnp.exp(draws), extent[position] // shards_of).reshape((-1,) + (1,) * (len(extent) - position - 1))

    loudness = one(*pieces[0])
    for cut in pieces[1:]:
        loudness = loudness * one(*cut)
    return loudness


def bell_draw(key, extent, spread, most, shards=(), kind=jnp.bfloat16):
    loudness = levels(key, extent, shards, -0.22, 0.18) if shards else 1.0
    result = jax.random.normal(key, extent, jnp.float32) * spread * loudness
    return jnp.minimum(jnp.maximum(result, -most), most).astype(kind)


def setup_inputs(seed: int = 0) -> dict:
    streams_of = jax.random.split(jax.random.key(seed), 5)
    return {
        "member_values": bell_draw(streams_of[0], (MEMBERS, OBS), 1.0, 6.0, ((0, 8), (1, 32)), jnp.float32),
        "obs_value": bell_draw(streams_of[1], (OBS,), 1.0, 6.0, ((0, 32),), jnp.float32),
        "obs_weight": jnp.clip(jnp.exp(math.log(4.0) - 2.7725887 * jax.random.uniform(streams_of[2], (OBS,), jnp.float32) ** levels(streams_of[2], (OBS,), ((0, 32),), -0.2, 0.2)), 0.25, 4.0),
        "obs_cell": draw_obs_cell(jax.random.fold_in(streams_of[4], 71), 0),
    }


def reference(member_values, obs_value, obs_weight, obs_cell):
    live = obs_cell >= 0
    weight = jnp.where(live, obs_weight, jnp.float32(0.0))
    cell_ids = jnp.where(live, obs_cell, 0).astype(jnp.int32)
    filled_flag = live.astype(jnp.float32)
    columns = jnp.concatenate([member_values * weight[None, :], (weight * obs_value)[None, :], weight[None, :], filled_flag[None, :]], 0)
    cell_sums = jax.vmap(lambda single: jax.ops.segment_sum(single, cell_ids, num_segments=CELLS))(columns)
    counted = cell_sums[MEMBERS + 2]
    filled = counted > 0
    weight_total = jnp.where(filled, cell_sums[MEMBERS + 1], jnp.float32(1.0))
    superob = cell_sums[:MEMBERS] / weight_total[None, :]
    observed_mean = cell_sums[MEMBERS] / weight_total
    ens_mean = jnp.sum(superob, 0) / MEMBERS
    deviation = superob - ens_mean[None, :]
    variance = jnp.sum(deviation * deviation, 0) / (MEMBERS - 1)
    departure = observed_mean - ens_mean
    error_variance = jnp.where(filled, 1.0 / weight_total, jnp.float32(0.0))
    return deviation, departure, variance, error_variance, counted.astype(jnp.int32)
```

```python
import functools

import jax
import jax.numpy as jnp
from jax import lax
from jax.experimental import pallas as pl
from jax.experimental.pallas import tpu as pltpu
from jax.sharding import PartitionSpec as P

CELL_DEV = 1920
LO = 256
HI = 8
ROWS = 16
PIECES = 3
GROUP = 4
MESH = pl.DeviceIdType.MESH


def kernel(
    regions, zs, members, cap,
    mem_hbm, val_hbm, wgt_hbm, cell_hbm,
    dev_ref, dep_ref, var_ref, err_ref, cnt_ref,
    mem_buf, v_buf, w_buf, c_buf, acc, stat, keep, zbuf,
    send_sem, recv_sem, zsend_sem, zrecv_sem,
):
    lanes = cap // 128
    me = lax.axis_index("reg")
    z = lax.axis_index("mem")
    core, col, row = me % 2, (me // 2) % 4, me // 8

    def peer(k):
        return ((row + k // 8) % 4) * 8 + ((col + (k // 2) % 4) % 4) * 2 + (core + k % 2) % 2

    barrier = pltpu.get_barrier_semaphore()

    def greet(k, _):
        pl.semaphore_signal(barrier, inc=1, device_id={"reg": peer(k)}, device_id_type=MESH)
        return 0

    lax.fori_loop(1, regions, greet, 0)

    def greet_z(j, _):
        pl.semaphore_signal(barrier, inc=1, device_id={"mem": (z + j) % zs}, device_id_type=MESH)
        return 0

    lax.fori_loop(1, zs, greet_z, 0)

    def pieces_of(k, to):
        columns = pl.ds(pl.multiple_of(to * cap, cap), cap)
        return (
            (mem_hbm.at[:, columns], mem_buf.at[k]),
            (val_hbm.at[to], v_buf.at[k]),
            (wgt_hbm.at[to], w_buf.at[k]),
            (cell_hbm.at[to], c_buf.at[k]),
        )

    own = [
        pltpu.make_async_copy(src, dst, recv_sem.at[i, 0])
        for i, (src, dst) in enumerate(pieces_of(0, me))
    ]
    for copy in own:
        copy.start()
    acc[...] = jnp.zeros_like(acc)
    pl.semaphore_wait(barrier, regions + zs - 2)

    def remote(k):
        to = peer(k)
        return [
            pltpu.make_async_remote_copy(
                src_ref=src, dst_ref=dst,
                send_sem=send_sem.at[i, k], recv_sem=recv_sem.at[i, k],
                device_id={"reg": to}, device_id_type=MESH,
            )
            for i, (src, dst) in enumerate(pieces_of(k, to))
        ]

    def send(k, _):
        for copy in remote(k)[::-1]:
            copy.start()
        return 0

    lax.fori_loop(1, regions, send, 0)

    base = me * CELL_DEV
    row_id = lax.broadcasted_iota(jnp.int32, (8, 128), 0)
    iota16 = lax.broadcasted_iota(jnp.int32, (16, 128), 0)
    one = jnp.ones((16, 128), jnp.bfloat16)
    zero = jnp.zeros((16, 128), jnp.bfloat16)
    lo_ids = [(iota16 + 16 * t).astype(jnp.float32).astype(jnp.bfloat16) for t in range(LO // 16)]

    def slot(k):
        left, right = [], []
        for a in range(lanes):
            at = pl.ds(a * 128, 128)
            w = jnp.broadcast_to(w_buf[k, pl.ds(a, 1), :], (8, 128))
            v = jnp.broadcast_to(v_buf[k, pl.ds(a, 1), :], (8, 128))
            c = jnp.broadcast_to(c_buf[k, pl.ds(a, 1), :], (16, 128)) - base
            top = mem_buf[k, pl.ds(0, 8), at] * w
            low = jnp.concatenate([mem_buf[k, pl.ds(8, members - 8), at], jnp.zeros((16 - members, 128), jnp.float32)], 0) * w
            low = jnp.where(row_id == 2, w, jnp.where(row_id == 3, 1.0, jnp.where(row_id == 4, w * v, low)))
            low = jnp.where(row_id < 5, low, 0.0)
            both = jnp.concatenate([top, low], 0)
            parts = []
            for p in range(PIECES):
                part = both.astype(jnp.bfloat16)
                parts.append(part)
                both = both - part.astype(jnp.float32)
            hi = (c >> 8).astype(jnp.float32).astype(jnp.bfloat16)
            lo = (c & 255).astype(jnp.float32).astype(jnp.bfloat16)
            masks = [hi == jnp.bfloat16(h) for h in range(HI)]
            left.append(jnp.concatenate([jnp.where(m, part, zero) for part in parts for m in masks], 0))
            right.append(jnp.concatenate([jnp.where(lo == ids, one, zero) for ids in lo_ids], 0))
        return left, right

    def group(g, _):
        left, right = [], []
        for j in range(GROUP):
            k = g * GROUP + j

            @pl.when(k == 0)
            def _():
                for copy in own:
                    copy.wait()

            @pl.when(k > 0)
            def _():
                for copy in remote(k):
                    copy.wait_recv()

            a, b = slot(k)
            left += a
            right += b
        acc[...] += lax.dot_general(
            jnp.concatenate(left, 1), jnp.concatenate(right, 1),
            (((1,), (1,)), ((), ())), preferred_element_type=jnp.float32,
        )
        return 0

    lax.fori_loop(0, regions // GROUP, group, 0)

    step = HI * ROWS
    sums = acc[pl.ds(0, step), :]
    for p in range(1, PIECES):
        sums = sums + acc[pl.ds(p * step, step), :]
    rows8 = lax.broadcasted_iota(jnp.int32, (8, LO), 0)
    for h in range(HI):
        top = sums[h * ROWS : h * ROWS + 8]
        low = sums[h * ROWS + 8 : h * ROWS + 16]
        weight, count, value = low[2:3], low[3:4], low[4:5]
        total = jnp.where(count > 0, weight, 1.0)
        top = top / total
        low = jnp.where(rows8 < members - 8, low / total, 0.0)
        one_sum = jnp.sum(top + low, 0, keepdims=True)
        mean = one_sum / members
        d_top = top - mean
        d_low = jnp.where(rows8 < members - 8, low - mean, 0.0)
        two = jnp.sum(d_top * d_top + d_low * d_low, 0, keepdims=True)
        for q in range(LO // 128):
            r = h * (LO // 128) + q
            cut = slice(q * 128, q * 128 + 128)
            stat[0, pl.ds(r, 1), :] = one_sum[:, cut]
            stat[1, pl.ds(r, 1), :] = two[:, cut]
            keep[0, pl.ds(r, 1), :] = total[:, cut]
            keep[1, pl.ds(r, 1), :] = count[:, cut]
            keep[2, pl.ds(r, 1), :] = value[:, cut]
            if r * 128 < CELL_DEV:
                dev_ref[pl.ds(0, 8), pl.ds(r * 128, 128)] = top[:, cut]
                dev_ref[pl.ds(8, members - 8), pl.ds(r * 128, 128)] = low[: members - 8, cut]

    def remote_z(j):
        return pltpu.make_async_remote_copy(
            src_ref=stat, dst_ref=zbuf.at[j],
            send_sem=zsend_sem.at[j], recv_sem=zrecv_sem.at[j],
            device_id={"mem": (z + j) % zs}, device_id_type=MESH,
        )

    for j in range(1, zs):
        remote_z(j).start()
    for j in range(1, zs):
        remote_z(j).wait_recv()

    firsts = [stat[0]] + [zbuf[j, 0] for j in range(1, zs)]
    seconds = [stat[1]] + [zbuf[j, 1] for j in range(1, zs)]
    ensemble = members * zs
    mean = functools.reduce(jnp.add, firsts) / ensemble
    spread = functools.reduce(jnp.add, seconds)
    for first in firsts:
        off = first / members - mean
        spread = spread + members * (off * off)
    n_rows = CELL_DEV // 128
    total, count = keep[0], keep[1]
    filled = count > 0
    departure = keep[2] / total - mean
    variance = spread / (ensemble - 1)
    error = jnp.where(filled, 1.0 / total, 0.0)
    dep_ref[...] = departure[:n_rows]
    var_ref[...] = variance[:n_rows]
    err_ref[...] = error[:n_rows]
    cnt_ref[...] = count.astype(jnp.int32)[:n_rows]
    for r in range(n_rows):
        at = pl.ds(r * 128, 128)
        dev_ref[:, at] = dev_ref[:, at] - mean[r : r + 1]

    def drain(k, _):
        for copy in remote(k):
            copy.wait_send()
        return 0

    lax.fori_loop(1, regions, drain, 0)
    for j in range(1, zs):
        remote_z(j).wait_send()


def shards(member_values, obs_value, obs_weight, obs_cell):
    regions = lax.axis_size("reg")
    zs = lax.axis_size("mem")
    members, obs = member_values.shape
    cap = obs // regions
    blocks = (regions, cap // 128, 128)
    n_rows = CELL_DEV // 128
    flat = jax.ShapeDtypeStruct((n_rows, 128), jnp.float32)
    any_spec = pl.BlockSpec(memory_space=pl.ANY)
    vmem = pl.BlockSpec(memory_space=pltpu.VMEM)
    dev, dep, var, err, cnt = pl.pallas_call(
        functools.partial(kernel, regions, zs, members, cap),
        out_shape=(
            jax.ShapeDtypeStruct((members, CELL_DEV), jnp.float32),
            flat, flat, flat,
            jax.ShapeDtypeStruct((n_rows, 128), jnp.int32),
        ),
        in_specs=[any_spec] * 4,
        out_specs=(vmem,) * 5,
        scratch_shapes=[
            pltpu.VMEM((regions, members, cap), jnp.float32),
            pltpu.VMEM(blocks, jnp.float32),
            pltpu.VMEM(blocks, jnp.float32),
            pltpu.VMEM(blocks, jnp.int32),
            pltpu.VMEM((PIECES * HI * ROWS, LO), jnp.float32),
            pltpu.VMEM((2, 16, 128), jnp.float32),
            pltpu.VMEM((3, 16, 128), jnp.float32),
            pltpu.VMEM((zs, 2, 16, 128), jnp.float32),
            pltpu.SemaphoreType.DMA((4, regions)),
            pltpu.SemaphoreType.DMA((4, regions)),
            pltpu.SemaphoreType.DMA((zs,)),
            pltpu.SemaphoreType.DMA((zs,)),
        ],
        compiler_params=pltpu.CompilerParams(collective_id=0, has_side_effects=True),
        name="superob",
    )(
        member_values,
        obs_value.reshape(blocks),
        obs_weight.reshape(blocks),
        obs_cell.reshape(blocks),
    )
    return dev, dep.reshape(-1), var.reshape(-1), err.reshape(-1), cnt.reshape(-1)


def solution(mesh):
    return jax.shard_map(
        shards,
        mesh=mesh,
        in_specs=(P("mem", "reg"), P("reg"), P("reg"), P("reg")),
        out_specs=(P("mem", "reg"), P("reg"), P("reg"), P("reg"), P("reg")),
        check_vma=False,
    )
```

```python
import functools

import jax
import jax.numpy as jnp
from jax import lax
from jax.experimental import pallas as pl
from jax.experimental.pallas import tpu as pltpu
from jax.sharding import PartitionSpec as P

CELL_DEV = 1920
LO = 256
HI = 8
ROWS = 16
PIECES = 3
GROUP = 4
MESH = pl.DeviceIdType.MESH


def kernel(
    regions, zs, members, cap,
    mem_hbm, val_hbm, wgt_hbm, cell_hbm,
    dev_ref, dep_ref, var_ref, err_ref, cnt_ref,
    mem_buf, ext_src, ext_buf, c_buf, acc, stat, keep, zbuf,
    stage_sem, send_sem, recv_sem, zsend_sem, zrecv_sem,
):
    lanes = cap // 128
    me = lax.axis_index("reg")
    z = lax.axis_index("mem")
    core, col, row = me % 2, (me // 2) % 4, me // 8

    def peer(k):
        return ((row + k // 8) % 4) * 8 + ((col + (k // 2) % 4) % 4) * 2 + (core + k % 2) % 2

    barrier = pltpu.get_barrier_semaphore()

    def greet(k, _):
        pl.semaphore_signal(barrier, inc=1, device_id={"reg": peer(k)}, device_id_type=MESH)
        return 0

    lax.fori_loop(1, regions, greet, 0)

    def greet_z(j, _):
        pl.semaphore_signal(barrier, inc=1, device_id={"mem": (z + j) % zs}, device_id_type=MESH)
        return 0

    lax.fori_loop(1, zs, greet_z, 0)

    def pieces_of(k, to):
        columns = pl.ds(pl.multiple_of(to * cap, cap), cap)
        return (
            (mem_hbm.at[pl.ds(0, 8), columns], mem_buf.at[k]),
            (ext_src.at[to], ext_buf.at[k]),
            (cell_hbm.at[to], c_buf.at[k]),
        )

    def stage(r):
        columns = pl.ds(pl.multiple_of(r * cap, cap), cap)
        return pltpu.make_async_copy(
            mem_hbm.at[pl.ds(8, members - 8), columns],
            ext_src.at[r, pl.ds(0, members - 8)],
            stage_sem.at[r],
        )

    extra = [
        pltpu.make_async_copy(src, ext_src.at[:, pl.ds(at, 1), :], stage_sem.at[regions + i])
        for i, (src, at) in enumerate(((wgt_hbm, members - 8), (val_hbm, members - 7)))
    ]
    for copy in extra:
        copy.start()

    def start_stage(r, _):
        stage(r).start()
        return 0

    def wait_stage(r, _):
        stage(r).wait()
        return 0

    lax.fori_loop(0, regions, start_stage, 0)
    acc[...] = jnp.zeros_like(acc)
    lax.fori_loop(0, regions, wait_stage, 0)
    for copy in extra:
        copy.wait()
    own = [
        pltpu.make_async_copy(src, dst, recv_sem.at[i, 0])
        for i, (src, dst) in enumerate(pieces_of(0, me))
    ]
    for copy in own:
        copy.start()
    pl.semaphore_wait(barrier, regions + zs - 2)

    def remote(k):
        to = peer(k)
        return [
            pltpu.make_async_remote_copy(
                src_ref=src, dst_ref=dst,
                send_sem=send_sem.at[i, k], recv_sem=recv_sem.at[i, k],
                device_id={"reg": to}, device_id_type=MESH,
            )
            for i, (src, dst) in enumerate(pieces_of(k, to))
        ]

    def send(k, _):
        for copy in remote(k)[::-1]:
            copy.start()
        return 0

    lax.fori_loop(1, regions, send, 0)

    base = me * CELL_DEV
    row_id = lax.broadcasted_iota(jnp.int32, (8, 128), 0)
    iota16 = lax.broadcasted_iota(jnp.int32, (16, 128), 0)
    one = jnp.ones((16, 128), jnp.bfloat16)
    zero = jnp.zeros((16, 128), jnp.bfloat16)
    lo_ids = [(iota16 + 16 * t).astype(jnp.float32).astype(jnp.bfloat16) for t in range(LO // 16)]

    def slot(k):
        left, right = [], []
        for a in range(lanes):
            at = pl.ds(a * 128, 128)
            w = jnp.broadcast_to(ext_buf[k, pl.ds(members - 8, 1), at], (8, 128))
            v = jnp.broadcast_to(ext_buf[k, pl.ds(members - 7, 1), at], (8, 128))
            c = jnp.broadcast_to(c_buf[k, pl.ds(a, 1), :], (16, 128)) - base
            top = mem_buf[k, pl.ds(0, 8), at] * w
            low = jnp.concatenate([ext_buf[k, pl.ds(0, members - 8), at], jnp.zeros((16 - members, 128), jnp.float32)], 0) * w
            low = jnp.where(row_id == 2, w, jnp.where(row_id == 3, 1.0, jnp.where(row_id == 4, w * v, low)))
            low = jnp.where(row_id < 5, low, 0.0)
            both = jnp.concatenate([top, low], 0)
            parts = []
            for p in range(PIECES):
                part = both.astype(jnp.bfloat16)
                parts.append(part)
                both = both - part.astype(jnp.float32)
            hi = (c >> 8).astype(jnp.float32).astype(jnp.bfloat16)
            lo = (c & 255).astype(jnp.float32).astype(jnp.bfloat16)
            masks = [hi == jnp.bfloat16(h) for h in range(HI)]
            left.append(jnp.concatenate([jnp.where(m, part, zero) for part in parts for m in masks], 0))
            right.append(jnp.concatenate([jnp.where(lo == ids, one, zero) for ids in lo_ids], 0))
        return left, right

    def group(g, _):
        left, right = [], []
        for j in range(GROUP):
            k = g * GROUP + j

            @pl.when(k == 0)
            def _():
                for copy in own:
                    copy.wait()

            @pl.when(k > 0)
            def _():
                for copy in remote(k):
                    copy.wait_recv()

            a, b = slot(k)
            left += a
            right += b
        acc[...] += lax.dot_general(
            jnp.concatenate(left, 1), jnp.concatenate(right, 1),
            (((1,), (1,)), ((), ())), preferred_element_type=jnp.float32,
        )
        return 0

    lax.fori_loop(0, regions // GROUP, group, 0)

    step = HI * ROWS
    sums = acc[pl.ds(0, step), :]
    for p in range(1, PIECES):
        sums = sums + acc[pl.ds(p * step, step), :]
    rows8 = lax.broadcasted_iota(jnp.int32, (8, LO), 0)
    for h in range(HI):
        top = sums[h * ROWS : h * ROWS + 8]
        low = sums[h * ROWS + 8 : h * ROWS + 16]
        weight, count, value = low[2:3], low[3:4], low[4:5]
        total = jnp.where(count > 0, weight, 1.0)
        top = top / total
        low = jnp.where(rows8 < members - 8, low / total, 0.0)
        one_sum = jnp.sum(top + low, 0, keepdims=True)
        mean = one_sum / members
        d_top = top - mean
        d_low = jnp.where(rows8 < members - 8, low - mean, 0.0)
        two = jnp.sum(d_top * d_top + d_low * d_low, 0, keepdims=True)
        for q in range(LO // 128):
            r = h * (LO // 128) + q
            cut = slice(q * 128, q * 128 + 128)
            stat[0, pl.ds(r, 1), :] = one_sum[:, cut]
            stat[1, pl.ds(r, 1), :] = two[:, cut]
            keep[0, pl.ds(r, 1), :] = total[:, cut]
            keep[1, pl.ds(r, 1), :] = count[:, cut]
            keep[2, pl.ds(r, 1), :] = value[:, cut]
            if r * 128 < CELL_DEV:
                dev_ref[pl.ds(0, 8), pl.ds(r * 128, 128)] = top[:, cut]
                dev_ref[pl.ds(8, members - 8), pl.ds(r * 128, 128)] = low[: members - 8, cut]

    def remote_z(j):
        return pltpu.make_async_remote_copy(
            src_ref=stat, dst_ref=zbuf.at[j],
            send_sem=zsend_sem.at[j], recv_sem=zrecv_sem.at[j],
            device_id={"mem": (z + j) % zs}, device_id_type=MESH,
        )

    for j in range(1, zs):
        remote_z(j).start()
    for j in range(1, zs):
        remote_z(j).wait_recv()

    firsts = [stat[0]] + [zbuf[j, 0] for j in range(1, zs)]
    seconds = [stat[1]] + [zbuf[j, 1] for j in range(1, zs)]
    ensemble = members * zs
    mean = functools.reduce(jnp.add, firsts) / ensemble
    spread = functools.reduce(jnp.add, seconds)
    for first in firsts:
        off = first / members - mean
        spread = spread + members * (off * off)
    n_rows = CELL_DEV // 128
    total, count = keep[0], keep[1]
    filled = count > 0
    departure = keep[2] / total - mean
    variance = spread / (ensemble - 1)
    error = jnp.where(filled, 1.0 / total, 0.0)
    dep_ref[...] = departure[:n_rows]
    var_ref[...] = variance[:n_rows]
    err_ref[...] = error[:n_rows]
    cnt_ref[...] = count.astype(jnp.int32)[:n_rows]
    for r in range(n_rows):
        at = pl.ds(r * 128, 128)
        dev_ref[:, at] = dev_ref[:, at] - mean[r : r + 1]

    def drain(k, _):
        for copy in remote(k):
            copy.wait_send()
        return 0

    lax.fori_loop(1, regions, drain, 0)
    for j in range(1, zs):
        remote_z(j).wait_send()


def settle(dev_in, dep_in, var_in, err_in, cnt_in, dev, dep, var, err, cnt):
    for src, dst in ((dev_in, dev), (dep_in, dep), (var_in, var), (err_in, err), (cnt_in, cnt)):
        dst[...] = src[...]


def shards(member_values, obs_value, obs_weight, obs_cell):
    regions = lax.axis_size("reg")
    zs = lax.axis_size("mem")
    members, obs = member_values.shape
    cap = obs // regions
    blocks = (regions, cap // 128, 128)
    n_rows = CELL_DEV // 128
    flat = jax.ShapeDtypeStruct((n_rows, 128), jnp.float32)
    any_spec = pl.BlockSpec(memory_space=pl.ANY)
    vmem = pl.BlockSpec(memory_space=pltpu.VMEM)
    shapes = (
        jax.ShapeDtypeStruct((members, CELL_DEV), jnp.float32),
        flat, flat, flat,
        jax.ShapeDtypeStruct((n_rows, 128), jnp.int32),
    )
    results = pl.pallas_call(
        functools.partial(kernel, regions, zs, members, cap),
        out_shape=shapes,
        in_specs=[any_spec] * 4,
        out_specs=(vmem,) * 5,
        scratch_shapes=[
            pltpu.VMEM((regions, 8, cap), jnp.float32),
            pltpu.VMEM((regions, members - 6, cap), jnp.float32),
            pltpu.VMEM((regions, members - 6, cap), jnp.float32),
            pltpu.VMEM(blocks, jnp.int32),
            pltpu.VMEM((PIECES * HI * ROWS, LO), jnp.float32),
            pltpu.VMEM((2, 16, 128), jnp.float32),
            pltpu.VMEM((3, 16, 128), jnp.float32),
            pltpu.VMEM((zs, 2, 16, 128), jnp.float32),
            pltpu.SemaphoreType.DMA((regions + 2,)),
            pltpu.SemaphoreType.DMA((3, regions)),
            pltpu.SemaphoreType.DMA((3, regions)),
            pltpu.SemaphoreType.DMA((zs,)),
            pltpu.SemaphoreType.DMA((zs,)),
        ],
        compiler_params=pltpu.CompilerParams(collective_id=0, has_side_effects=True, vmem_limit_bytes=8 << 20),
        name="superob",
    )(
        *(
            pltpu.with_memory_space_constraint(a, pltpu.HBM)
            for a in (
                member_values,
                obs_value.reshape(regions, 1, cap),
                obs_weight.reshape(regions, 1, cap),
                obs_cell.reshape(blocks),
            )
        )
    )
    dev, dep, var, err, cnt = pl.pallas_call(
        settle, out_shape=shapes, in_specs=[vmem] * 5, out_specs=(vmem,) * 5, name="settle",
        compiler_params=pltpu.CompilerParams(vmem_limit_bytes=1 << 20),
    )(*results)
    return dev, dep.reshape(-1), var.reshape(-1), err.reshape(-1), cnt.reshape(-1)


def solution(mesh):
    return jax.shard_map(
        shards,
        mesh=mesh,
        in_specs=(P("mem", "reg"), P("reg"), P("reg"), P("reg")),
        out_specs=(P("mem", "reg"), P("reg"), P("reg"), P("reg"), P("reg")),
        check_vma=False,
    )
```

```python
import functools

import jax
import jax.numpy as jnp
from jax import lax
from jax.experimental import pallas as pl
from jax.experimental.pallas import tpu as pltpu
from jax.sharding import PartitionSpec as P

CELL_DEV = 1920
LO = 256
HI = 8
ROWS = 16
PIECES = 3
GROUP = 4
MESH = pl.DeviceIdType.MESH


def hops(shift):
    return sum(min(d, 4 - d) for d in shift[:2])


SHIFTS = sorted(
    ((dy, dx, dc) for dc in range(2) for dy in range(4) for dx in range(4) if dy or dx or dc),
    key=hops,
)
GROUPS = (4,) * 8


def kernel(
    regions, zs, members, cap,
    mem_hbm, val_hbm, wgt_hbm, cell_hbm,
    dev_ref, dep_ref, var_ref, err_ref, cnt_ref,
    mem_buf, ext_src, ext_buf, c_buf, acc, stat, keep, zbuf,
    stage_sem, send_sem, recv_sem, zsend_sem, zrecv_sem,
):
    lanes = cap // 128
    me = lax.axis_index("reg")
    z = lax.axis_index("mem")
    core, col, row = me % 2, (me // 2) % 4, me // 8

    def peer(shift):
        dy, dx, dc = shift
        return ((row + dy) % 4) * 8 + ((col + dx) % 4) * 2 + (core + dc) % 2

    barrier = pltpu.get_barrier_semaphore()

    for j in sorted(range(1, zs), key=lambda j: -min(j, zs - j)):
        pl.semaphore_signal(barrier, inc=1, device_id={"mem": (z + j) % zs}, device_id_type=MESH)
    peers = [peer(shift) for shift in SHIFTS]
    for to in peers:
        pl.semaphore_signal(barrier, inc=1, device_id={"reg": to}, device_id_type=MESH)

    def pieces_of(k, to):
        columns = pl.ds(pl.multiple_of(to * cap, cap), cap)
        return (
            (mem_hbm.at[pl.ds(0, 8), columns], mem_buf.at[k]),
            (ext_src.at[to], ext_buf.at[k]),
            (cell_hbm.at[to], c_buf.at[k]),
        )

    def stage(r):
        columns = pl.ds(pl.multiple_of(r * cap, cap), cap)
        return pltpu.make_async_copy(
            mem_hbm.at[pl.ds(8, members - 8), columns],
            ext_src.at[r, pl.ds(0, members - 8)],
            stage_sem.at[r],
        )

    extra = [
        pltpu.make_async_copy(src, ext_src.at[:, pl.ds(at, 1), :], stage_sem.at[regions + i])
        for i, (src, at) in enumerate(((wgt_hbm, members - 8), (val_hbm, members - 7)))
    ]
    for copy in extra:
        copy.start()

    def start_stage(r, _):
        stage(r).start()
        return 0

    def wait_stage(r, _):
        stage(r).wait()
        return 0

    lax.fori_loop(0, regions, start_stage, 0)
    acc[...] = jnp.zeros_like(acc)
    lax.fori_loop(0, regions, wait_stage, 0)
    for copy in extra:
        copy.wait()
    own = [
        pltpu.make_async_copy(src, dst, recv_sem.at[i, 0])
        for i, (src, dst) in enumerate(pieces_of(0, me))
    ]
    for copy in own:
        copy.start()
    pl.semaphore_wait(barrier, regions + zs - 2)

    def remote(k, to):
        return [
            pltpu.make_async_remote_copy(
                src_ref=src, dst_ref=dst,
                send_sem=send_sem.at[i, k], recv_sem=recv_sem.at[i, k],
                device_id={"reg": to}, device_id_type=MESH,
            )
            for i, (src, dst) in enumerate(pieces_of(k, to))
        ]

    for k, to in enumerate(peers):
        for copy in remote(k + 1, to)[::-1]:
            copy.start()

    base = me * CELL_DEV
    row_id = lax.broadcasted_iota(jnp.int32, (8, 128), 0)
    iota16 = lax.broadcasted_iota(jnp.int32, (16, 128), 0)
    one = jnp.ones((16, 128), jnp.bfloat16)
    zero = jnp.zeros((16, 128), jnp.bfloat16)
    lo_ids = [(iota16 + 16 * t).astype(jnp.float32).astype(jnp.bfloat16) for t in range(LO // 16)]

    def slot(k):
        left, right = [], []
        for a in range(lanes):
            at = pl.ds(a * 128, 128)
            w = jnp.broadcast_to(ext_buf[k, pl.ds(members - 8, 1), at], (8, 128))
            v = jnp.broadcast_to(ext_buf[k, pl.ds(members - 7, 1), at], (8, 128))
            c = jnp.broadcast_to(c_buf[k, pl.ds(a, 1), :], (16, 128)) - base
            top = mem_buf[k, pl.ds(0, 8), at] * w
            low = jnp.concatenate([ext_buf[k, pl.ds(0, members - 8), at], jnp.zeros((16 - members, 128), jnp.float32)], 0) * w
            low = jnp.where(row_id == 2, w, jnp.where(row_id == 3, 1.0, jnp.where(row_id == 4, w * v, low)))
            low = jnp.where(row_id < 5, low, 0.0)
            both = jnp.concatenate([top, low], 0)
            parts = []
            for p in range(PIECES):
                part = both.astype(jnp.bfloat16)
                parts.append(part)
                both = both - part.astype(jnp.float32)
            hi = (c >> 8).astype(jnp.float32).astype(jnp.bfloat16)
            lo = (c & 255).astype(jnp.float32).astype(jnp.bfloat16)
            masks = [hi == jnp.bfloat16(h) for h in range(HI)]
            left.append(jnp.concatenate([jnp.where(m, part, zero) for part in parts for m in masks], 0))
            right.append(jnp.concatenate([jnp.where(lo == ids, one, zero) for ids in lo_ids], 0))
        return left, right

    def arrived(k):
        for copy in remote(k, peers[-1]):
            copy.wait_recv()

    def add(slots):
        left, right = [], []
        for k in slots:
            a, b = slot(k)
            left += a
            right += b
        acc[...] += lax.dot_general(
            jnp.concatenate(left, 1), jnp.concatenate(right, 1),
            (((1,), (1,)), ((), ())), preferred_element_type=jnp.float32,
        )

    for copy in own:
        copy.wait()
    for k in range(1, GROUPS[0]):
        arrived(k)
    add(range(GROUPS[0]))
    same = sum(1 for size in GROUPS if size == GROUP)

    def group(g, _):
        slots = [g * GROUP + j for j in range(GROUP)]
        for k in slots:
            arrived(k)
        add(slots)
        return 0

    lax.fori_loop(1, same, group, 0)
    at = same * GROUP
    for size in GROUPS[same:]:
        for k in range(at, at + size):
            arrived(k)
        add(range(at, at + size))
        at += size

    step = HI * ROWS
    sums = acc[pl.ds(0, step), :]
    for p in range(1, PIECES):
        sums = sums + acc[pl.ds(p * step, step), :]
    rows8 = lax.broadcasted_iota(jnp.int32, (8, LO), 0)
    for h in range(HI):
        top = sums[h * ROWS : h * ROWS + 8]
        low = sums[h * ROWS + 8 : h * ROWS + 16]
        weight, count, value = low[2:3], low[3:4], low[4:5]
        total = jnp.where(count > 0, weight, 1.0)
        top = top / total
        low = jnp.where(rows8 < members - 8, low / total, 0.0)
        one_sum = jnp.sum(top + low, 0, keepdims=True)
        mean = one_sum / members
        d_top = top - mean
        d_low = jnp.where(rows8 < members - 8, low - mean, 0.0)
        two = jnp.sum(d_top * d_top + d_low * d_low, 0, keepdims=True)
        for q in range(LO // 128):
            r = h * (LO // 128) + q
            cut = slice(q * 128, q * 128 + 128)
            stat[0, pl.ds(r, 1), :] = one_sum[:, cut]
            stat[1, pl.ds(r, 1), :] = two[:, cut]
            keep[0, pl.ds(r, 1), :] = total[:, cut]
            keep[1, pl.ds(r, 1), :] = count[:, cut]
            keep[2, pl.ds(r, 1), :] = value[:, cut]
            if r * 128 < CELL_DEV:
                dev_ref[pl.ds(0, 8), pl.ds(r * 128, 128)] = top[:, cut]
                dev_ref[pl.ds(8, members - 8), pl.ds(r * 128, 128)] = low[: members - 8, cut]

    def remote_z(j):
        return pltpu.make_async_remote_copy(
            src_ref=stat, dst_ref=zbuf.at[j],
            send_sem=zsend_sem.at[j], recv_sem=zrecv_sem.at[j],
            device_id={"mem": (z + j) % zs}, device_id_type=MESH,
        )

    for j in range(1, zs):
        remote_z(j).start()
    for k, to in enumerate(peers):
        for copy in remote(k + 1, to):
            copy.wait_send()
    for j in range(1, zs):
        remote_z(j).wait_recv()

    firsts = [stat[0]] + [zbuf[j, 0] for j in range(1, zs)]
    seconds = [stat[1]] + [zbuf[j, 1] for j in range(1, zs)]
    ensemble = members * zs
    mean = functools.reduce(jnp.add, firsts) / ensemble
    spread = functools.reduce(jnp.add, seconds)
    for first in firsts:
        off = first / members - mean
        spread = spread + members * (off * off)
    n_rows = CELL_DEV // 128
    total, count = keep[0], keep[1]
    filled = count > 0
    departure = keep[2] / total - mean
    variance = spread / (ensemble - 1)
    error = jnp.where(filled, 1.0 / total, 0.0)
    dep_ref[...] = departure[:n_rows]
    var_ref[...] = variance[:n_rows]
    err_ref[...] = error[:n_rows]
    cnt_ref[...] = count.astype(jnp.int32)[:n_rows]
    for r in range(n_rows):
        at = pl.ds(r * 128, 128)
        dev_ref[:, at] = dev_ref[:, at] - mean[r : r + 1]

    for j in range(1, zs):
        remote_z(j).wait_send()


def settle(dev_in, dep_in, var_in, err_in, cnt_in, dev, dep, var, err, cnt):
    for src, dst in ((dev_in, dev), (dep_in, dep), (var_in, var), (err_in, err), (cnt_in, cnt)):
        dst[...] = src[...]


def shards(member_values, obs_value, obs_weight, obs_cell):
    regions = lax.axis_size("reg")
    zs = lax.axis_size("mem")
    members, obs = member_values.shape
    cap = obs // regions
    blocks = (regions, cap // 128, 128)
    n_rows = CELL_DEV // 128
    flat = jax.ShapeDtypeStruct((n_rows, 128), jnp.float32)
    any_spec = pl.BlockSpec(memory_space=pl.ANY)
    vmem = pl.BlockSpec(memory_space=pltpu.VMEM)
    shapes = (
        jax.ShapeDtypeStruct((members, CELL_DEV), jnp.float32),
        flat, flat, flat,
        jax.ShapeDtypeStruct((n_rows, 128), jnp.int32),
    )
    results = pl.pallas_call(
        functools.partial(kernel, regions, zs, members, cap),
        out_shape=shapes,
        in_specs=[any_spec] * 4,
        out_specs=(vmem,) * 5,
        scratch_shapes=[
            pltpu.VMEM((regions, 8, cap), jnp.float32),
            pltpu.VMEM((regions, members - 6, cap), jnp.float32),
            pltpu.VMEM((regions, members - 6, cap), jnp.float32),
            pltpu.VMEM(blocks, jnp.int32),
            pltpu.VMEM((PIECES * HI * ROWS, LO), jnp.float32),
            pltpu.VMEM((2, 16, 128), jnp.float32),
            pltpu.VMEM((3, 16, 128), jnp.float32),
            pltpu.VMEM((zs, 2, 16, 128), jnp.float32),
            pltpu.SemaphoreType.DMA((regions + 2,)),
            pltpu.SemaphoreType.DMA((3, regions)),
            pltpu.SemaphoreType.DMA((3, regions)),
            pltpu.SemaphoreType.DMA((zs,)),
            pltpu.SemaphoreType.DMA((zs,)),
        ],
        compiler_params=pltpu.CompilerParams(collective_id=0, has_side_effects=True, vmem_limit_bytes=8 << 20),
        name="superob",
    )(
        *(
            pltpu.with_memory_space_constraint(a, pltpu.HBM)
            for a in (
                member_values,
                obs_value.reshape(regions, 1, cap),
                obs_weight.reshape(regions, 1, cap),
                obs_cell.reshape(blocks),
            )
        )
    )
    dev, dep, var, err, cnt = pl.pallas_call(
        settle, out_shape=shapes, in_specs=[vmem] * 5, out_specs=(vmem,) * 5, name="settle",
        compiler_params=pltpu.CompilerParams(vmem_limit_bytes=1 << 20),
    )(*results)
    return dev, dep.reshape(-1), var.reshape(-1), err.reshape(-1), cnt.reshape(-1)


def solution(mesh):
    return jax.shard_map(
        shards,
        mesh=mesh,
        in_specs=(P("mem", "reg"), P("reg"), P("reg"), P("reg")),
        out_specs=(P("mem", "reg"), P("reg"), P("reg"), P("reg"), P("reg")),
        check_vma=False,
    )
```

```python
import functools

import jax
import jax.numpy as jnp
from jax import lax
from jax.experimental import pallas as pl
from jax.experimental.pallas import tpu as pltpu
from jax.sharding import PartitionSpec as P

CELL_DEV = 1920
LO = 256
HI = 8
ROWS = 16
PIECES = 3
GROUP = 4
MESH = pl.DeviceIdType.MESH


def hops(shift):
    return sum(min(d, 4 - d) for d in shift[:2])


SHIFTS = sorted(
    ((dy, dx, dc) for dc in range(2) for dy in range(4) for dx in range(4) if dy or dx or dc),
    key=hops,
)
GROUPS = (4,) * 8


def kernel(
    regions, zs, members, cap,
    mem_hbm, val_hbm, wgt_hbm, cell_hbm,
    dev_ref, mean_ref, dep_ref, var_ref, err_ref, cnt_ref,
    mem_buf, mem_src, ext_src, ext_buf, v_buf, c_src, acc, stat, keep, obs, zbuf,
    stage_sem, send_sem, recv_sem, zsend_sem, zrecv_sem, osend_sem, orecv_sem, zreply,
):
    lanes = cap // 128
    me = lax.axis_index("reg")
    z = lax.axis_index("mem")
    core, col, row = me % 2, (me // 2) % 4, me // 8

    def peer(shift):
        dy, dx, dc = shift
        return ((row + dy) % 4) * 8 + ((col + dx) % 4) * 2 + (core + dc) % 2

    barrier = pltpu.get_barrier_semaphore()

    peers = [peer(shift) for shift in SHIFTS]
    for to in peers[::-1]:
        pl.semaphore_signal(barrier, inc=1, device_id={"reg": to}, device_id_type=MESH)
    zpeers = [(z + j) % zs for j in range(1, zs)]
    zahead = [z < other for other in zpeers]
    for to, early in zip(zpeers, zahead):
        @pl.when(early)
        def _():
            pl.semaphore_signal(barrier, inc=1, device_id={"mem": to}, device_id_type=MESH)

    def pieces_of(k, to):
        columns = pl.ds(pl.multiple_of(to * cap, cap), cap)
        return (
            (mem_src.at[:, columns], mem_buf.at[k]),
            (ext_src.at[to], ext_buf.at[k]),
            (val_hbm.at[to], v_buf.at[k]),
        )

    def stage(r):
        columns = pl.ds(pl.multiple_of(r * cap, cap), cap)
        return pltpu.make_async_copy(
            mem_hbm.at[pl.ds(8, members - 8), columns],
            ext_src.at[r, pl.ds(0, members - 8)],
            stage_sem.at[r],
        )

    cell_copy = pltpu.make_async_copy(cell_hbm, c_src, stage_sem.at[regions + 1])
    cell_copy.start()
    main_copy = pltpu.make_async_copy(mem_hbm.at[pl.ds(0, 8), :], mem_src, stage_sem.at[regions + 2])
    main_copy.start()
    extra = [
        pltpu.make_async_copy(
            wgt_hbm, ext_src.at[:, pl.ds(members - 8, 1), :], stage_sem.at[regions]
        )
    ]
    for copy in extra:
        copy.start()

    def start_stage(r, _):
        stage(r).start()
        return 0

    def wait_stage(r, _):
        stage(r).wait()
        return 0

    lax.fori_loop(0, regions, start_stage, 0)
    acc[...] = jnp.zeros_like(acc)
    cell_copy.wait()

    def place_cell(r, _):
        ext_src[r, pl.ds(members - 7, 1), :] = c_src[r].astype(jnp.float32)
        return 0

    lax.fori_loop(0, regions, place_cell, 0, unroll=8)
    lax.fori_loop(0, regions, wait_stage, 0)
    main_copy.wait()
    for copy in extra:
        copy.wait()
    own = [
        pltpu.make_async_copy(src, dst, recv_sem.at[i, 0])
        for i, (src, dst) in enumerate(pieces_of(0, me))
    ]
    for copy in own:
        copy.start()
    pl.semaphore_wait(barrier, regions - 1 + z)

    first = z == 0

    def remote(k, to, which):
        pieces = pieces_of(k, to)
        return [
            pltpu.make_async_remote_copy(
                src_ref=src, dst_ref=dst,
                send_sem=send_sem.at[i, k], recv_sem=recv_sem.at[i, k],
                device_id={"reg": to}, device_id_type=MESH,
            )
            for i in which
            for src, dst in [pieces[i]]
        ]

    @pl.when(first)
    def _():
        for k, to in enumerate(peers):
            remote(k + 1, to, (2,))[0].start()

    for k, to in enumerate(peers):
        main, ext = remote(k + 1, to, (0, 1))
        ext.start()
        main.start()

    for j, (to, early) in enumerate(zip(zpeers, zahead)):
        @pl.when(jnp.logical_not(early))
        def _():
            pl.semaphore_signal(zreply.at[zs - 2 - j], inc=1, device_id={"mem": to}, device_id_type=MESH)

    base = me * CELL_DEV
    row_id = lax.broadcasted_iota(jnp.int32, (8, 128), 0)
    iota16 = lax.broadcasted_iota(jnp.int32, (16, 128), 0)
    one = jnp.ones((16, 128), jnp.bfloat16)
    zero = jnp.zeros((16, 128), jnp.bfloat16)
    lo_ids = [(iota16 + 16 * t).astype(jnp.float32).astype(jnp.bfloat16) for t in range(LO // 16)]

    def slot(k):
        left, right = [], []
        for a in range(lanes):
            at = pl.ds(a * 128, 128)
            w = jnp.broadcast_to(ext_buf[k, pl.ds(members - 8, 1), at], (8, 128))
            v = jnp.broadcast_to(v_buf[k, :, at], (8, 128))
            c = jnp.broadcast_to(ext_buf[k, pl.ds(members - 7, 1), at].astype(jnp.int32), (16, 128)) - base
            top = mem_buf[k, pl.ds(0, 8), at] * w
            low = jnp.concatenate([ext_buf[k, pl.ds(0, members - 8), at], jnp.zeros((16 - members, 128), jnp.float32)], 0) * w
            low = jnp.where(row_id == 2, w, jnp.where(row_id == 3, 1.0, jnp.where((row_id == 4) & first, w * v, low)))
            low = jnp.where(row_id < 5, low, 0.0)
            both = jnp.concatenate([top, low], 0)
            parts = []
            for p in range(PIECES):
                part = both.astype(jnp.bfloat16)
                parts.append(part)
                both = both - part.astype(jnp.float32)
            hi = (c >> 8).astype(jnp.float32).astype(jnp.bfloat16)
            lo = (c & 255).astype(jnp.float32).astype(jnp.bfloat16)
            masks = [hi == jnp.bfloat16(h) for h in range(HI)]
            left.append(jnp.concatenate([jnp.where(m, part, zero) for part in parts for m in masks], 0))
            right.append(jnp.concatenate([jnp.where(lo == ids, one, zero) for ids in lo_ids], 0))
        return left, right

    def arrived(k):
        main, ext = remote(k, peers[-1], (0, 1))
        ext.wait_recv()
        main.wait_recv()

        @pl.when(first)
        def _():
            remote(k, peers[-1], (2,))[0].wait_recv()

    def add(slots):
        left, right = [], []
        for k in slots:
            a, b = slot(k)
            left += a
            right += b
        acc[...] += lax.dot_general(
            jnp.concatenate(left, 1), jnp.concatenate(right, 1),
            (((1,), (1,)), ((), ())), preferred_element_type=jnp.float32,
        )

    for copy in own:
        copy.wait()
    for k in range(1, GROUPS[0]):
        arrived(k)
    add(range(GROUPS[0]))
    same = sum(1 for size in GROUPS if size == GROUP)

    def group(g, _):
        slots = [g * GROUP + j for j in range(GROUP)]
        for k in slots:
            arrived(k)
        add(slots)
        return 0

    lax.fori_loop(1, same, group, 0)
    at = same * GROUP
    for size in GROUPS[same:]:
        for k in range(at, at + size):
            arrived(k)
        add(range(at, at + size))
        at += size

    step = HI * ROWS
    sums = acc[pl.ds(0, step), :]
    for p in range(1, PIECES):
        sums = sums + acc[pl.ds(p * step, step), :]
    rows8 = lax.broadcasted_iota(jnp.int32, (8, LO), 0)
    for h in range(HI):
        top = sums[h * ROWS : h * ROWS + 8]
        low = sums[h * ROWS + 8 : h * ROWS + 16]
        weight, count, value = low[2:3], low[3:4], low[4:5]
        total = jnp.where(count > 0, weight, 1.0)
        top = top / total
        low = jnp.where(rows8 < members - 8, low / total, 0.0)
        one_sum = jnp.sum(top + low, 0, keepdims=True)
        mean = one_sum / members
        d_top = top - mean
        d_low = jnp.where(rows8 < members - 8, low - mean, 0.0)
        two = jnp.sum(d_top * d_top + d_low * d_low, 0, keepdims=True)
        for q in range(LO // 128):
            r = h * (LO // 128) + q
            cut = slice(q * 128, q * 128 + 128)
            stat[0, pl.ds(r, 1), :] = one_sum[:, cut]
            stat[1, pl.ds(r, 1), :] = two[:, cut]
            keep[0, pl.ds(r, 1), :] = total[:, cut]
            keep[1, pl.ds(r, 1), :] = count[:, cut]

            @pl.when(first)
            def _():
                obs[pl.ds(r, 1), :] = value[:, cut]

            if r * 128 < CELL_DEV:
                dev_ref[pl.ds(0, 8), pl.ds(r * 128, 128)] = top[:, cut]
                dev_ref[pl.ds(8, members - 8), pl.ds(r * 128, 128)] = low[: members - 8, cut]

    def remote_z(j):
        return pltpu.make_async_remote_copy(
            src_ref=stat, dst_ref=zbuf.at[j],
            send_sem=zsend_sem.at[j], recv_sem=zrecv_sem.at[j],
            device_id={"mem": (z + j) % zs}, device_id_type=MESH,
        )

    def remote_obs(j):
        return pltpu.make_async_remote_copy(
            src_ref=obs, dst_ref=obs,
            send_sem=osend_sem.at[j], recv_sem=orecv_sem.at[0],
            device_id={"mem": (z + j) % zs}, device_id_type=MESH,
        )

    for j in range(zs - 1):
        @pl.when(zahead[j])
        def _():
            pl.semaphore_wait(zreply.at[j], 1)

    for j in sorted(range(1, zs), key=lambda j: -min(j, zs - j)):
        remote_z(j).start()

    @pl.when(first)
    def _():
        for j in range(1, zs):
            remote_obs(j).start()

    for k, to in enumerate(peers):
        for copy in remote(k + 1, to, (0, 1)):
            copy.wait_send()

    @pl.when(first)
    def _():
        for k, to in enumerate(peers):
            remote(k + 1, to, (2,))[0].wait_send()
        for j in range(1, zs):
            remote_obs(j).wait_send()

    @pl.when(jnp.logical_not(first))
    def _():
        remote_obs(1).wait_recv()

    for j in range(1, zs):
        remote_z(j).wait_recv()

    firsts = [stat[0]] + [zbuf[j, 0] for j in range(1, zs)]
    seconds = [stat[1]] + [zbuf[j, 1] for j in range(1, zs)]
    ensemble = members * zs
    mean = functools.reduce(jnp.add, firsts) / ensemble
    spread = functools.reduce(jnp.add, seconds)
    for first in firsts:
        off = first / members - mean
        spread = spread + members * (off * off)
    n_rows = CELL_DEV // 128
    total, count = keep[0], keep[1]
    filled = count > 0
    departure = obs[...] / total - mean
    variance = spread / (ensemble - 1)
    error = jnp.where(filled, 1.0 / total, 0.0)
    dep_ref[...] = departure[:n_rows]
    var_ref[...] = variance[:n_rows]
    err_ref[...] = error[:n_rows]
    cnt_ref[...] = count.astype(jnp.int32)[:n_rows]
    mean_ref[...] = mean[:n_rows]

    for j in range(1, zs):
        remote_z(j).wait_send()


def settle(sup_in, mean_in, dep_in, var_in, err_in, cnt_in, dev, dep, var, err, cnt):
    for src, dst in ((dep_in, dep), (var_in, var), (err_in, err), (cnt_in, cnt)):
        dst[...] = src[...]
    for r in range(CELL_DEV // 128):
        at = pl.ds(r * 128, 128)
        dev[:, at] = sup_in[:, at] - mean_in[pl.ds(r, 1), :]


def shards(member_values, obs_value, obs_weight, obs_cell):
    regions = lax.axis_size("reg")
    zs = lax.axis_size("mem")
    members, obs = member_values.shape
    cap = obs // regions
    n_rows = CELL_DEV // 128
    flat = jax.ShapeDtypeStruct((n_rows, 128), jnp.float32)
    any_spec = pl.BlockSpec(memory_space=pl.ANY)
    vmem = pl.BlockSpec(memory_space=pltpu.VMEM)
    shapes = (
        jax.ShapeDtypeStruct((members, CELL_DEV), jnp.float32),
        flat, flat, flat,
        jax.ShapeDtypeStruct((n_rows, 128), jnp.int32),
    )
    results = pl.pallas_call(
        functools.partial(kernel, regions, zs, members, cap),
        out_shape=(shapes[0], flat, *shapes[1:]),
        in_specs=[any_spec] * 4,
        out_specs=(vmem,) * 6,
        scratch_shapes=[
            pltpu.VMEM((regions, 8, cap), jnp.float32),
            pltpu.VMEM((8, regions * cap), jnp.float32),
            pltpu.VMEM((regions, members - 6, cap), jnp.float32),
            pltpu.VMEM((regions, members - 6, cap), jnp.float32),
            pltpu.VMEM((regions, 1, cap), jnp.float32),
            pltpu.VMEM((regions, 1, cap), jnp.int32),
            pltpu.VMEM((PIECES * HI * ROWS, LO), jnp.float32),
            pltpu.VMEM((2, 16, 128), jnp.float32),
            pltpu.VMEM((2, 16, 128), jnp.float32),
            pltpu.VMEM((16, 128), jnp.float32),
            pltpu.VMEM((zs, 2, 16, 128), jnp.float32),
            pltpu.SemaphoreType.DMA((regions + 3,)),
            pltpu.SemaphoreType.DMA((3, regions)),
            pltpu.SemaphoreType.DMA((3, regions)),
            pltpu.SemaphoreType.DMA((zs,)),
            pltpu.SemaphoreType.DMA((zs,)),
            pltpu.SemaphoreType.DMA((zs,)),
            pltpu.SemaphoreType.DMA((1,)),
            pltpu.SemaphoreType.REGULAR((zs - 1,)),
        ],
        compiler_params=pltpu.CompilerParams(collective_id=0, has_side_effects=True, vmem_limit_bytes=8 << 20),
        name="superob",
    )(
        *(
            pltpu.with_memory_space_constraint(a, pltpu.HBM)
            for a in (
                member_values,
                obs_value.reshape(regions, 1, cap),
                obs_weight.reshape(regions, 1, cap),
                obs_cell.reshape(regions, 1, cap),
            )
        )
    )
    dev, dep, var, err, cnt = pl.pallas_call(
        settle, out_shape=shapes, in_specs=[vmem] * 6, out_specs=(vmem,) * 5, name="settle",
        compiler_params=pltpu.CompilerParams(vmem_limit_bytes=1 << 20),
    )(*results)
    return dev, dep.reshape(-1), var.reshape(-1), err.reshape(-1), cnt.reshape(-1)


def solution(mesh):
    return jax.shard_map(
        shards,
        mesh=mesh,
        in_specs=(P("mem", "reg"), P("reg"), P("reg"), P("reg")),
        out_specs=(P("mem", "reg"), P("reg"), P("reg"), P("reg"), P("reg")),
        check_vma=False,
    )
```

```python
import functools

import jax
import jax.numpy as jnp
from jax import lax
from jax.experimental import pallas as pl
from jax.experimental.pallas import tpu as pltpu
from jax.sharding import PartitionSpec as P

CELL_DEV = 1920
LO = 256
HI = 8
ROWS = 16
PIECES = 3
GROUP = 4
MESH = pl.DeviceIdType.MESH


def hops(shift):
    return sum(min(d, 4 - d) for d in shift[:2])


SHIFTS = sorted(
    ((dy, dx, dc) for dc in range(2) for dy in range(4) for dx in range(4) if dy or dx or dc),
    key=hops,
)


def kernel(
    regions, zs, members, cap,
    mem_hbm, val_hbm, wgt_hbm, cell_hbm,
    dev_ref, mean_ref, dep_ref, var_ref, err_ref, cnt_ref,
    mem_buf, mem_src, ext_src, ext_buf, v_buf, c_src, acc, stat, keep, obs, zbuf,
    stage_sem, send_sem, recv_sem, zsend_sem, zrecv_sem, osend_sem, orecv_sem, zreply,
):
    lanes = cap // 128
    me = lax.axis_index("reg")
    z = lax.axis_index("mem")
    core, col, row = me % 2, (me // 2) % 4, me // 8

    def peer(shift):
        dy, dx, dc = shift
        return ((row + dy) % 4) * 8 + ((col + dx) % 4) * 2 + (core + dc) % 2

    barrier = pltpu.get_barrier_semaphore()

    peers = [peer(shift) for shift in SHIFTS]
    def pieces_of(k, to):
        columns = pl.ds(pl.multiple_of(to * cap, cap), cap)
        return (
            (mem_src.at[:, columns], mem_buf.at[k]),
            (ext_src.at[:, columns], ext_buf.at[k]),
            (val_hbm.at[to], v_buf.at[k]),
        )

    spare = members - 8
    staged = [
        pltpu.make_async_copy(src, dst, stage_sem.at[i])
        for i, (src, dst) in enumerate(
            (
                (cell_hbm, c_src),
                (mem_hbm.at[pl.ds(0, 8), :], mem_src),
                (mem_hbm.at[pl.ds(8, spare), :], ext_src.at[pl.ds(0, spare), :]),
                (wgt_hbm, ext_src.at[pl.ds(spare, 1), :]),
            )
        )
    ]
    for copy in staged:
        copy.start()
    for to in peers[::-1]:
        pl.semaphore_signal(barrier, inc=1, device_id={"reg": to}, device_id_type=MESH)
    zpeers = [(z + j) % zs for j in range(1, zs)]
    zahead = [z < other for other in zpeers]
    for to, early in zip(zpeers, zahead):
        @pl.when(early)
        def _():
            pl.semaphore_signal(barrier, inc=1, device_id={"mem": to}, device_id_type=MESH)

    acc[...] = jnp.zeros_like(acc)
    staged[0].wait()
    ext_src[pl.ds(spare + 1, 1), :] = c_src[...].astype(jnp.float32)
    for copy in staged[1:]:
        copy.wait()
    own = [
        pltpu.make_async_copy(src, dst, recv_sem.at[i, 0])
        for i, (src, dst) in enumerate(pieces_of(0, me))
    ]
    for copy in own:
        copy.start()
    pl.semaphore_wait(barrier, regions - 1 + z)

    first = z == 0

    def remote(k, to, which):
        pieces = pieces_of(k, to)
        return [
            pltpu.make_async_remote_copy(
                src_ref=src, dst_ref=dst,
                send_sem=send_sem.at[i, k], recv_sem=recv_sem.at[i, k],
                device_id={"reg": to}, device_id_type=MESH,
            )
            for i in which
            for src, dst in [pieces[i]]
        ]

    @pl.when(first)
    def _():
        for k, to in enumerate(peers):
            remote(k + 1, to, (2,))[0].start()

    for k, to in enumerate(peers):
        main, ext = remote(k + 1, to, (0, 1))
        ext.start()
        main.start()

    for j, (to, early) in enumerate(zip(zpeers, zahead)):
        @pl.when(jnp.logical_not(early))
        def _():
            pl.semaphore_signal(zreply.at[zs - 2 - j], inc=1, device_id={"mem": to}, device_id_type=MESH)

    base = me * CELL_DEV
    row_id = lax.broadcasted_iota(jnp.int32, (8, 128), 0)
    iota16 = lax.broadcasted_iota(jnp.int32, (16, 128), 0)
    one = jnp.ones((16, 128), jnp.bfloat16)
    zero = jnp.zeros((16, 128), jnp.bfloat16)
    lo_ids = [(iota16 + 16 * t).astype(jnp.float32).astype(jnp.bfloat16) for t in range(LO // 16)]

    def slot(k):
        left, right = [], []
        for a in range(lanes):
            at = pl.ds(a * 128, 128)
            w = jnp.broadcast_to(ext_buf[k, pl.ds(members - 8, 1), at], (8, 128))
            v = jnp.broadcast_to(v_buf[k, :, at], (8, 128))
            c = jnp.broadcast_to(ext_buf[k, pl.ds(members - 7, 1), at].astype(jnp.int32), (16, 128)) - base
            top = mem_buf[k, pl.ds(0, 8), at] * w
            low = jnp.concatenate([ext_buf[k, pl.ds(0, members - 8), at], jnp.zeros((16 - members, 128), jnp.float32)], 0) * w
            low = jnp.where(row_id == 2, w, jnp.where(row_id == 3, 1.0, jnp.where((row_id == 4) & first, w * v, low)))
            low = jnp.where(row_id < 5, low, 0.0)
            both = jnp.concatenate([top, low], 0)
            parts = []
            for p in range(PIECES):
                part = both.astype(jnp.bfloat16)
                parts.append(part)
                both = both - part.astype(jnp.float32)
            hi = (c >> 8).astype(jnp.float32).astype(jnp.bfloat16)
            lo = (c & 255).astype(jnp.float32).astype(jnp.bfloat16)
            masks = [hi == jnp.bfloat16(h) for h in range(HI)]
            left.append(jnp.concatenate([jnp.where(m, part, zero) for part in parts for m in masks], 0))
            right.append(jnp.concatenate([jnp.where(lo == ids, one, zero) for ids in lo_ids], 0))
        return left, right

    def arrived(k):
        main, ext = remote(k, peers[-1], (0, 1))
        ext.wait_recv()
        main.wait_recv()

        @pl.when(first)
        def _():
            remote(k, peers[-1], (2,))[0].wait_recv()

    def add(slots):
        left, right = [], []
        for k in slots:
            a, b = slot(k)
            left += a
            right += b
        acc[...] += lax.dot_general(
            jnp.concatenate(left, 1), jnp.concatenate(right, 1),
            (((1,), (1,)), ((), ())), preferred_element_type=jnp.float32,
        )

    for copy in own:
        copy.wait()

    def group(g, _):
        slots = [g * GROUP + j for j in range(GROUP)]

        @pl.when(g == 0)
        def _():
            for k in range(1, GROUP):
                arrived(k)

        @pl.when(g > 0)
        def _():
            for k in slots:
                arrived(k)

        add(slots)
        return 0

    lax.fori_loop(0, regions // GROUP, group, 0)

    step = HI * ROWS
    rows8 = lax.broadcasted_iota(jnp.int32, (8, LO), 0)

    def band(h, _):
        def rows(off):
            at = pl.multiple_of(h * ROWS + off, 8)
            return sum(acc[pl.ds(p * step + at, 8), :] for p in range(PIECES))

        top, low = rows(0), rows(8)
        weight, count, value = low[2:3], low[3:4], low[4:5]
        total = jnp.where(count > 0, weight, 1.0)
        top = top / total
        low = jnp.where(rows8 < members - 8, low / total, 0.0)
        one_sum = jnp.sum(top + low, 0, keepdims=True)
        mean = one_sum / members
        d_top = top - mean
        d_low = jnp.where(rows8 < members - 8, low - mean, 0.0)
        two = jnp.sum(d_top * d_top + d_low * d_low, 0, keepdims=True)
        cells = pl.ds(pl.multiple_of(h * LO, LO), LO)
        dev_ref[pl.ds(0, 8), cells] = top
        dev_ref[pl.ds(8, members - 8), cells] = low[: members - 8]
        for q in range(LO // 128):
            r = h * (LO // 128) + q
            cut = slice(q * 128, q * 128 + 128)
            stat[0, pl.ds(r, 1), :] = one_sum[:, cut]
            stat[1, pl.ds(r, 1), :] = two[:, cut]
            keep[0, pl.ds(r, 1), :] = total[:, cut]
            keep[1, pl.ds(r, 1), :] = count[:, cut]

            @pl.when(first)
            def _():
                obs[pl.ds(r, 1), :] = value[:, cut]

        return 0

    lax.fori_loop(0, HI, band, 0)

    def remote_z(j):
        return pltpu.make_async_remote_copy(
            src_ref=stat, dst_ref=zbuf.at[j],
            send_sem=zsend_sem.at[j], recv_sem=zrecv_sem.at[j],
            device_id={"mem": (z + j) % zs}, device_id_type=MESH,
        )

    def remote_obs(j):
        return pltpu.make_async_remote_copy(
            src_ref=obs, dst_ref=obs,
            send_sem=osend_sem.at[j], recv_sem=orecv_sem.at[0],
            device_id={"mem": (z + j) % zs}, device_id_type=MESH,
        )

    for j in range(zs - 1):
        @pl.when(zahead[j])
        def _():
            pl.semaphore_wait(zreply.at[j], 1)

    for j in sorted(range(1, zs), key=lambda j: -min(j, zs - j)):
        remote_z(j).start()

    @pl.when(first)
    def _():
        for j in range(1, zs):
            remote_obs(j).start()

    for k, to in enumerate(peers):
        for copy in remote(k + 1, to, (0, 1)):
            copy.wait_send()

    @pl.when(first)
    def _():
        for k, to in enumerate(peers):
            remote(k + 1, to, (2,))[0].wait_send()
        for j in range(1, zs):
            remote_obs(j).wait_send()

    @pl.when(jnp.logical_not(first))
    def _():
        remote_obs(1).wait_recv()

    for j in range(1, zs):
        remote_z(j).wait_recv()

    firsts = [stat[0]] + [zbuf[j, 0] for j in range(1, zs)]
    seconds = [stat[1]] + [zbuf[j, 1] for j in range(1, zs)]
    ensemble = members * zs
    mean = functools.reduce(jnp.add, firsts) / ensemble
    spread = functools.reduce(jnp.add, seconds)
    for first in firsts:
        off = first / members - mean
        spread = spread + members * (off * off)
    n_rows = CELL_DEV // 128
    total, count = keep[0], keep[1]
    filled = count > 0
    departure = obs[...] / total - mean
    variance = spread / (ensemble - 1)
    error = jnp.where(filled, 1.0 / total, 0.0)
    dep_ref[...] = departure[:n_rows]
    var_ref[...] = variance[:n_rows]
    err_ref[...] = error[:n_rows]
    cnt_ref[...] = count.astype(jnp.int32)[:n_rows]
    mean_ref[...] = mean[:n_rows]

    for j in range(1, zs):
        remote_z(j).wait_send()


def settle(sup_in, mean_in, dep_in, var_in, err_in, cnt_in, dev, dep, var, err, cnt):
    for src, dst in ((dep_in, dep), (var_in, var), (err_in, err), (cnt_in, cnt)):
        dst[...] = src[...]
    for r in range(CELL_DEV // 128):
        at = pl.ds(r * 128, 128)
        dev[:, at] = sup_in[:, at] - mean_in[pl.ds(r, 1), :]


def shards(member_values, obs_value, obs_weight, obs_cell):
    regions = lax.axis_size("reg")
    zs = lax.axis_size("mem")
    members, obs = member_values.shape
    cap = obs // regions
    n_rows = CELL_DEV // 128
    flat = jax.ShapeDtypeStruct((n_rows, 128), jnp.float32)
    any_spec = pl.BlockSpec(memory_space=pl.ANY)
    vmem = pl.BlockSpec(memory_space=pltpu.VMEM)
    shapes = (
        jax.ShapeDtypeStruct((members, CELL_DEV), jnp.float32),
        flat, flat, flat,
        jax.ShapeDtypeStruct((n_rows, 128), jnp.int32),
    )
    results = pl.pallas_call(
        functools.partial(kernel, regions, zs, members, cap),
        out_shape=(
            jax.ShapeDtypeStruct((members, HI * LO), jnp.float32), flat, *shapes[1:]
        ),
        in_specs=[any_spec] * 4,
        out_specs=(vmem,) * 6,
        scratch_shapes=[
            pltpu.VMEM((regions, 8, cap), jnp.float32),
            pltpu.VMEM((8, regions * cap), jnp.float32),
            pltpu.VMEM((members - 6, regions * cap), jnp.float32),
            pltpu.VMEM((regions, members - 6, cap), jnp.float32),
            pltpu.VMEM((regions, 1, cap), jnp.float32),
            pltpu.VMEM((1, regions * cap), jnp.int32),
            pltpu.VMEM((PIECES * HI * ROWS, LO), jnp.float32),
            pltpu.VMEM((2, 16, 128), jnp.float32),
            pltpu.VMEM((2, 16, 128), jnp.float32),
            pltpu.VMEM((16, 128), jnp.float32),
            pltpu.VMEM((zs, 2, 16, 128), jnp.float32),
            pltpu.SemaphoreType.DMA((4,)),
            pltpu.SemaphoreType.DMA((3, regions)),
            pltpu.SemaphoreType.DMA((3, regions)),
            pltpu.SemaphoreType.DMA((zs,)),
            pltpu.SemaphoreType.DMA((zs,)),
            pltpu.SemaphoreType.DMA((zs,)),
            pltpu.SemaphoreType.DMA((1,)),
            pltpu.SemaphoreType.REGULAR((zs - 1,)),
        ],
        compiler_params=pltpu.CompilerParams(collective_id=0, has_side_effects=True, vmem_limit_bytes=8 << 20),
        name="superob",
    )(
        *(
            pltpu.with_memory_space_constraint(a, pltpu.HBM)
            for a in (
                member_values,
                obs_value.reshape(regions, 1, cap),
                obs_weight.reshape(1, -1),
                obs_cell.reshape(1, -1),
            )
        )
    )
    dev, dep, var, err, cnt = pl.pallas_call(
        settle, out_shape=shapes, in_specs=[vmem] * 6, out_specs=(vmem,) * 5, name="settle",
        compiler_params=pltpu.CompilerParams(vmem_limit_bytes=1 << 20),
    )(*results)
    return dev, dep.reshape(-1), var.reshape(-1), err.reshape(-1), cnt.reshape(-1)


def solution(mesh):
    return jax.shard_map(
        shards,
        mesh=mesh,
        in_specs=(P("mem", "reg"), P("reg"), P("reg"), P("reg")),
        out_specs=(P("mem", "reg"), P("reg"), P("reg"), P("reg"), P("reg")),
        check_vma=False,
    )
```

```python
import functools

import jax
import jax.numpy as jnp
from jax import lax
from jax.experimental import pallas as pl
from jax.experimental.pallas import tpu as pltpu
from jax.sharding import PartitionSpec as P

CELL_DEV = 1920
LO = 256
HI = 8
ROWS = 16
PIECES = 3
GROUP = 4
MESH = pl.DeviceIdType.MESH


def hops(shift):
    return sum(min(d, 4 - d) for d in shift[:2])


SHIFTS = sorted(
    ((dy, dx, dc) for dc in range(2) for dy in range(4) for dx in range(4) if dy or dx or dc),
    key=lambda shift: (0, 1, 2, 4, 3).index(hops(shift)),
)


def kernel(
    regions, zs, members, cap,
    mem_hbm, val_hbm, wgt_hbm, cell_hbm,
    dev_ref, mean_ref, dep_ref, var_ref, err_ref, cnt_ref,
    mem_buf, mem_src, ext_src, ext_buf, v_buf, c_src, acc, stat, keep, obs, zbuf,
    stage_sem, send_sem, recv_sem, zsend_sem, zrecv_sem, osend_sem, orecv_sem, zreply,
):
    lanes = cap // 128
    me = lax.axis_index("reg")
    z = lax.axis_index("mem")
    core, col, row = me % 2, (me // 2) % 4, me // 8

    def peer(shift):
        dy, dx, dc = shift
        return ((row + dy) % 4) * 8 + ((col + dx) % 4) * 2 + (core + dc) % 2

    barrier = pltpu.get_barrier_semaphore()

    peers = [peer(shift) for shift in SHIFTS]
    def pieces_of(k, to):
        columns = pl.ds(pl.multiple_of(to * cap, cap), cap)
        return (
            (mem_src.at[:, columns], mem_buf.at[k]),
            (ext_src.at[:, columns], ext_buf.at[k]),
            (val_hbm.at[to], v_buf.at[k]),
        )

    spare = members - 8
    staged = [
        pltpu.make_async_copy(src, dst, stage_sem.at[i])
        for i, (src, dst) in enumerate(
            (
                (cell_hbm, c_src),
                (mem_hbm.at[pl.ds(0, 8), :], mem_src),
                (mem_hbm.at[pl.ds(8, spare), :], ext_src.at[pl.ds(0, spare), :]),
                (wgt_hbm, ext_src.at[pl.ds(spare, 1), :]),
            )
        )
    ]
    for copy in staged:
        copy.start()
    for to in peers[::-1]:
        pl.semaphore_signal(barrier, inc=1, device_id={"reg": to}, device_id_type=MESH)
    zpeers = [(z + j) % zs for j in range(1, zs)]
    zahead = [z < other for other in zpeers]
    for to, early in zip(zpeers, zahead):
        @pl.when(early)
        def _():
            pl.semaphore_signal(barrier, inc=1, device_id={"mem": to}, device_id_type=MESH)

    acc[...] = jnp.zeros_like(acc)
    staged[0].wait()
    ext_src[pl.ds(spare + 1, 1), :] = c_src[...].astype(jnp.float32)
    for copy in staged[1:]:
        copy.wait()
    own = [
        pltpu.make_async_copy(src, dst, recv_sem.at[i, 0])
        for i, (src, dst) in enumerate(pieces_of(0, me))
    ]
    for copy in own:
        copy.start()
    pl.semaphore_wait(barrier, regions - 1 + z)

    first = z == 0

    def remote(k, to, which):
        pieces = pieces_of(k, to)
        return [
            pltpu.make_async_remote_copy(
                src_ref=src, dst_ref=dst,
                send_sem=send_sem.at[i, k], recv_sem=recv_sem.at[i, k],
                device_id={"reg": to}, device_id_type=MESH,
            )
            for i in which
            for src, dst in [pieces[i]]
        ]

    @pl.when(first)
    def _():
        for k, to in enumerate(peers):
            remote(k + 1, to, (2,))[0].start()

    for k, to in enumerate(peers):
        main, ext = remote(k + 1, to, (0, 1))
        ext.start()
        main.start()

    for j, (to, early) in enumerate(zip(zpeers, zahead)):
        @pl.when(jnp.logical_not(early))
        def _():
            pl.semaphore_signal(zreply.at[zs - 2 - j], inc=1, device_id={"mem": to}, device_id_type=MESH)

    base = me * CELL_DEV
    row_id = lax.broadcasted_iota(jnp.int32, (8, 128), 0)
    iota16 = lax.broadcasted_iota(jnp.int32, (16, 128), 0)
    one = jnp.ones((16, 128), jnp.bfloat16)
    zero = jnp.zeros((16, 128), jnp.bfloat16)
    lo_ids = [(iota16 + 16 * t).astype(jnp.float32).astype(jnp.bfloat16) for t in range(LO // 16)]

    def slot(k):
        left, right = [], []
        for a in range(lanes):
            at = pl.ds(a * 128, 128)
            w = jnp.broadcast_to(ext_buf[k, pl.ds(members - 8, 1), at], (8, 128))
            v = jnp.broadcast_to(v_buf[k, :, at], (8, 128))
            c = jnp.broadcast_to(ext_buf[k, pl.ds(members - 7, 1), at].astype(jnp.int32), (16, 128)) - base
            top = mem_buf[k, pl.ds(0, 8), at] * w
            low = jnp.concatenate([ext_buf[k, pl.ds(0, members - 8), at], jnp.zeros((16 - members, 128), jnp.float32)], 0) * w
            low = jnp.where(row_id == 2, w, jnp.where(row_id == 3, 1.0, jnp.where((row_id == 4) & first, w * v, low)))
            low = jnp.where(row_id < 5, low, 0.0)
            both = jnp.concatenate([top, low], 0)
            parts = []
            for p in range(PIECES):
                part = both.astype(jnp.bfloat16)
                parts.append(part)
                both = both - part.astype(jnp.float32)
            hi = (c >> 8).astype(jnp.float32).astype(jnp.bfloat16)
            lo = (c & 255).astype(jnp.float32).astype(jnp.bfloat16)
            masks = [hi == jnp.bfloat16(h) for h in range(HI)]
            left.append(jnp.concatenate([jnp.where(m, part, zero) for part in parts for m in masks], 0))
            right.append(jnp.concatenate([jnp.where(lo == ids, one, zero) for ids in lo_ids], 0))
        return left, right

    def arrived(k):
        main, ext = remote(k, peers[-1], (0, 1))
        ext.wait_recv()
        main.wait_recv()

        @pl.when(first)
        def _():
            remote(k, peers[-1], (2,))[0].wait_recv()

    def add(slots):
        left, right = [], []
        for k in slots:
            a, b = slot(k)
            left += a
            right += b
        acc[...] += lax.dot_general(
            jnp.concatenate(left, 1), jnp.concatenate(right, 1),
            (((1,), (1,)), ((), ())), preferred_element_type=jnp.float32,
        )

    for copy in own:
        copy.wait()

    def group(g, _):
        slots = [g * GROUP + j for j in range(GROUP)]

        @pl.when(g == 0)
        def _():
            for k in range(1, GROUP):
                arrived(k)

        @pl.when(g > 0)
        def _():
            for k in slots:
                arrived(k)

        add(slots)
        return 0

    lax.fori_loop(0, regions // GROUP, group, 0)

    step = HI * ROWS
    rows8 = lax.broadcasted_iota(jnp.int32, (8, LO), 0)

    def band(h, _):
        def rows(off):
            at = pl.multiple_of(h * ROWS + off, 8)
            return sum(acc[pl.ds(p * step + at, 8), :] for p in range(PIECES))

        top, low = rows(0), rows(8)
        weight, count, value = low[2:3], low[3:4], low[4:5]
        total = jnp.where(count > 0, weight, 1.0)
        top = top / total
        low = jnp.where(rows8 < members - 8, low / total, 0.0)
        one_sum = jnp.sum(top + low, 0, keepdims=True)
        mean = one_sum / members
        d_top = top - mean
        d_low = jnp.where(rows8 < members - 8, low - mean, 0.0)
        two = jnp.sum(d_top * d_top + d_low * d_low, 0, keepdims=True)
        cells = pl.ds(pl.multiple_of(h * LO, LO), LO)
        dev_ref[pl.ds(0, 8), cells] = top
        dev_ref[pl.ds(8, members - 8), cells] = low[: members - 8]
        for q in range(LO // 128):
            r = h * (LO // 128) + q
            cut = slice(q * 128, q * 128 + 128)
            stat[0, pl.ds(r, 1), :] = one_sum[:, cut]
            stat[1, pl.ds(r, 1), :] = two[:, cut]
            keep[0, pl.ds(r, 1), :] = total[:, cut]
            keep[1, pl.ds(r, 1), :] = count[:, cut]

            @pl.when(first)
            def _():
                obs[pl.ds(r, 1), :] = value[:, cut]

        return 0

    lax.fori_loop(0, HI, band, 0)

    def remote_z(j):
        return pltpu.make_async_remote_copy(
            src_ref=stat, dst_ref=zbuf.at[j],
            send_sem=zsend_sem.at[j], recv_sem=zrecv_sem.at[j],
            device_id={"mem": (z + j) % zs}, device_id_type=MESH,
        )

    def remote_obs(j):
        return pltpu.make_async_remote_copy(
            src_ref=obs, dst_ref=obs,
            send_sem=osend_sem.at[j], recv_sem=orecv_sem.at[0],
            device_id={"mem": (z + j) % zs}, device_id_type=MESH,
        )

    for j in range(zs - 1):
        @pl.when(zahead[j])
        def _():
            pl.semaphore_wait(zreply.at[j], 1)

    for j in sorted(range(1, zs), key=lambda j: -min(j, zs - j)):
        remote_z(j).start()

    @pl.when(first)
    def _():
        for j in range(1, zs):
            remote_obs(j).start()

    for k, to in enumerate(peers):
        for copy in remote(k + 1, to, (0, 1)):
            copy.wait_send()

    @pl.when(first)
    def _():
        for k, to in enumerate(peers):
            remote(k + 1, to, (2,))[0].wait_send()
        for j in range(1, zs):
            remote_obs(j).wait_send()

    @pl.when(jnp.logical_not(first))
    def _():
        remote_obs(1).wait_recv()

    for j in range(1, zs):
        remote_z(j).wait_recv()

    firsts = [stat[0]] + [zbuf[j, 0] for j in range(1, zs)]
    seconds = [stat[1]] + [zbuf[j, 1] for j in range(1, zs)]
    ensemble = members * zs
    mean = functools.reduce(jnp.add, firsts) / ensemble
    spread = functools.reduce(jnp.add, seconds)
    for first in firsts:
        off = first / members - mean
        spread = spread + members * (off * off)
    n_rows = CELL_DEV // 128
    total, count = keep[0], keep[1]
    filled = count > 0
    departure = obs[...] / total - mean
    variance = spread / (ensemble - 1)
    error = jnp.where(filled, 1.0 / total, 0.0)
    dep_ref[...] = departure[:n_rows]
    var_ref[...] = variance[:n_rows]
    err_ref[...] = error[:n_rows]
    cnt_ref[...] = count.astype(jnp.int32)[:n_rows]
    mean_ref[...] = mean[:n_rows]

    for j in range(1, zs):
        remote_z(j).wait_send()


def settle(sup_in, mean_in, dep_in, var_in, err_in, cnt_in, dev, dep, var, err, cnt):
    for src, dst in ((dep_in, dep), (var_in, var), (err_in, err), (cnt_in, cnt)):
        dst[...] = src[...]
    for r in range(CELL_DEV // 128):
        at = pl.ds(r * 128, 128)
        dev[:, at] = sup_in[:, at] - mean_in[pl.ds(r, 1), :]


def shards(member_values, obs_value, obs_weight, obs_cell):
    regions = lax.axis_size("reg")
    zs = lax.axis_size("mem")
    members, obs = member_values.shape
    cap = obs // regions
    n_rows = CELL_DEV // 128
    flat = jax.ShapeDtypeStruct((n_rows, 128), jnp.float32)
    any_spec = pl.BlockSpec(memory_space=pl.ANY)
    vmem = pl.BlockSpec(memory_space=pltpu.VMEM)
    shapes = (
        jax.ShapeDtypeStruct((members, CELL_DEV), jnp.float32),
        flat, flat, flat,
        jax.ShapeDtypeStruct((n_rows, 128), jnp.int32),
    )
    results = pl.pallas_call(
        functools.partial(kernel, regions, zs, members, cap),
        out_shape=(
            jax.ShapeDtypeStruct((members, HI * LO), jnp.float32), flat, *shapes[1:]
        ),
        in_specs=[any_spec] * 4,
        out_specs=(vmem,) * 6,
        scratch_shapes=[
            pltpu.VMEM((regions, 8, cap), jnp.float32),
            pltpu.VMEM((8, regions * cap), jnp.float32),
            pltpu.VMEM((members - 6, regions * cap), jnp.float32),
            pltpu.VMEM((regions, members - 6, cap), jnp.float32),
            pltpu.VMEM((regions, 1, cap), jnp.float32),
            pltpu.VMEM((1, regions * cap), jnp.int32),
            pltpu.VMEM((PIECES * HI * ROWS, LO), jnp.float32),
            pltpu.VMEM((2, 16, 128), jnp.float32),
            pltpu.VMEM((2, 16, 128), jnp.float32),
            pltpu.VMEM((16, 128), jnp.float32),
            pltpu.VMEM((zs, 2, 16, 128), jnp.float32),
            pltpu.SemaphoreType.DMA((4,)),
            pltpu.SemaphoreType.DMA((3, regions)),
            pltpu.SemaphoreType.DMA((3, regions)),
            pltpu.SemaphoreType.DMA((zs,)),
            pltpu.SemaphoreType.DMA((zs,)),
            pltpu.SemaphoreType.DMA((zs,)),
            pltpu.SemaphoreType.DMA((1,)),
            pltpu.SemaphoreType.REGULAR((zs - 1,)),
        ],
        compiler_params=pltpu.CompilerParams(collective_id=0, has_side_effects=True, vmem_limit_bytes=8 << 20),
        name="superob",
    )(
        *(
            pltpu.with_memory_space_constraint(a, pltpu.HBM)
            for a in (
                member_values,
                obs_value.reshape(regions, 1, cap),
                obs_weight.reshape(1, -1),
                obs_cell.reshape(1, -1),
            )
        )
    )
    dev, dep, var, err, cnt = pl.pallas_call(
        settle, out_shape=shapes, in_specs=[vmem] * 6, out_specs=(vmem,) * 5, name="settle",
        compiler_params=pltpu.CompilerParams(vmem_limit_bytes=1 << 20),
    )(*results)
    return dev, dep.reshape(-1), var.reshape(-1), err.reshape(-1), cnt.reshape(-1)


def solution(mesh):
    return jax.shard_map(
        shards,
        mesh=mesh,
        in_specs=(P("mem", "reg"), P("reg"), P("reg"), P("reg")),
        out_specs=(P("mem", "reg"), P("reg"), P("reg"), P("reg"), P("reg")),
        check_vma=False,
    )
```
